256 devices in a mesh: dp: 32 (over x, y, core), tensor: 8 (over z).
Axes of the slice: x: 4, y: 4, z: 8, core: 2. Of those that a mesh axis runs over, the one named last changes fastest.
Arguments:
- inputs: bfloat16 [32768, 8192], P('dp', 'tensor'), may hold values from -6 to 6
- frozen_value_weight: bfloat16 [8192, 1024], P('tensor'), may hold values from -0.0625 to 0.0625
- adapter_down_weight: bfloat16 [512, 8192, 64], P('dp', 'tensor'), may hold values from -0.0625 to 0.0625
- adapter_up_weight: bfloat16 [512, 64, 1024], P('dp', None, 'tensor'), may hold values from -0.75 to 0.75
- adapter_per_block: int32 [256], P('dp'), may hold values from 0 to 511, as said below
- adapter_storage_index: int32 [512], replicated, may hold values from 0 to 511, as said below
- value_gradient: bfloat16 [32768, 1024], P('dp', 'tensor'), may hold values from -6 to 6
Outputs:
- values: bfloat16 [32768, 1024], P('dp', 'tensor')
- grad_inputs: bfloat16 [32768, 8192], P('dp', 'tensor')
- grad_down: bfloat16 [512, 8192, 64], P('dp', 'tensor')
- grad_up: bfloat16 [512, 64, 1024], P('dp', None, 'tensor')
The draws below stay inside these ranges and needn't reach their ends.
Inputs may be any that keep to these rules, and one draw needn't show every extreme that they name: Adapter a is kept by data device adapter_storage_index[a] // 16; adapter_storage_index is a permutation. `adapter_per_block`: the 8 blocks of one data device use adapters kept by pairwise different data devices; in every draw there is one data device whose adapters are used by a block of every data device, so that keeper serves all 32 data devices.
All inputs are finite; a program needn't handle non-finite values.
Results may differ from the reference program's by a relative error of at most 0.0054.
Values may be sent and summed in bfloat16 or wider, within the bound.
A program may use at most 128 MiB of HBM per device.

```python
import jax
import jax.numpy as jnp
from jax import lax

MODEL_WIDTH = 8192
VALUE_WIDTH = 1024
ADAPTER_RANK = 64
BLOCK = 128
ADP_DEV = 16
BLOCKS_DEV = 8
ADAPTER_TOTAL = 512
TOTAL_BLOCKS = 256
ROW_TOTAL = 32768


def layout(key):
    frozen_output = jax.random.fold_in(key, 11)
    k_perm, k_hot, k_noise, k_order, k_slot = jax.random.split(frozen_output, 5)
    owners_count = ADAPTER_TOTAL // ADP_DEV
    index = jax.random.permutation(k_perm, ADAPTER_TOTAL).astype(jnp.int32)
    hot = jax.random.randint(k_hot, (), 0, owners_count)
    owners = jnp.arange(owners_count, dtype=jnp.int32)
    noise = jax.random.randint(k_noise, (owners_count, owners_count), 0, 2 ** 20)
    score = noise * owners_count + owners[None, :] + jnp.where(owners[None, :] == hot, 2 ** 29, 0)
    chosen = jnp.argsort(-score, axis=1)[:, :BLOCKS_DEV].astype(jnp.int32)
    mixing = jax.random.randint(k_order, (owners_count, BLOCKS_DEV), 0, 2 ** 20) * BLOCKS_DEV + jnp.arange(BLOCKS_DEV, dtype=jnp.int32)[None, :]
    reorder = jnp.argsort(mixing, axis=1)
    chosen = jnp.take_along_axis(chosen, reorder, axis=1)
    slots = jax.random.randint(k_slot, (owners_count, BLOCKS_DEV), 0, ADP_DEV)
    spots = (chosen * ADP_DEV + slots).reshape(-1)
    inverse = jnp.argsort(index).astype(jnp.int32)
    return (index, inverse[spots].astype(jnp.int32))


def draw_adapter_storage_index(key, part):
    return layout(key)[0]


def draw_adapter_per_block(key, part):
    return layout(key)[1]


def steps_of(own_key, extent, pieces, low, high):
    factor_of = 1.0
    for dim, shards_of in pieces:
        heights = jax.random.uniform(jax.random.fold_in(jax.random.fold_in(own_key, 6), dim), (shards_of,), jnp.float32, low / len(pieces), high / len(pieces))
        factor_of = factor_of * jnp.repeat(jnp.exp(heights), extent[dim] // shards_of).reshape((-1,) + (1,) * (len(extent) - 1 - dim))
    return factor_of


def bell_draw(key, dims, width, limit, cuts=(), held_as=jnp.bfloat16):
    entries = width * jax.random.normal(key, dims, jnp.float32)
    if cuts:
        entries = entries * steps_of(key, dims, cuts, -0.22, 0.18)
    return jnp.clip(entries, -limit, limit).astype(held_as)


def setup_inputs(seed: int = 0) -> dict:
    arg_keys = jax.random.split(jax.random.key(seed), 8)
    inputs = bell_draw(arg_keys[0], (ROW_TOTAL, MODEL_WIDTH), 1.0, 6.0, ((0, 32), (1, 8)))
    frozen_value_weight = bell_draw(arg_keys[1], (MODEL_WIDTH, VALUE_WIDTH), MODEL_WIDTH ** -0.5, 0.0625, ((0, 8),))
    adapter_down_weight = bell_draw(arg_keys[2], (ADAPTER_TOTAL, MODEL_WIDTH, ADAPTER_RANK), MODEL_WIDTH ** -0.5, 0.0625, ((0, 32), (1, 8)))
    adapter_up_weight = bell_draw(arg_keys[3], (ADAPTER_TOTAL, ADAPTER_RANK, VALUE_WIDTH), ADAPTER_RANK ** -0.5, 0.75, ((0, 32), (2, 8)))
    adapter_per_block = draw_adapter_per_block(jax.random.fold_in(arg_keys[7], 71), 0)
    adapter_storage_index = draw_adapter_storage_index(jax.random.fold_in(arg_keys[7], 71), 0)
    value_gradient = bell_draw(arg_keys[6], (ROW_TOTAL, VALUE_WIDTH), 1.0, 6.0, ((0, 32), (1, 8)))
    return {"inputs": inputs, "frozen_value_weight": frozen_value_weight, "adapter_down_weight": adapter_down_weight, "adapter_up_weight": adapter_up_weight, "adapter_per_block": adapter_per_block, "adapter_storage_index": adapter_storage_index, "value_gradient": value_gradient}


adapter_scale = 0.5


def reference(inputs, frozen_value_weight, adapter_down_weight, adapter_up_weight, adapter_per_block, adapter_storage_index, value_gradient):
    spot = adapter_storage_index[adapter_per_block].astype(jnp.int32)
    x_blocks = inputs.reshape(TOTAL_BLOCKS, BLOCK, MODEL_WIDTH)
    dy_blocks = value_gradient.reshape(TOTAL_BLOCKS, BLOCK, VALUE_WIDTH)

    def step(carry, item):
        acc_down, acc_up = carry
        x_blk, output_gradient_block, row_position = item
        down_matrix = lax.dynamic_index_in_dim(adapter_down_weight, row_position, 0, keepdims=False)
        up_matrix = lax.dynamic_index_in_dim(adapter_up_weight, row_position, 0, keepdims=False)
        low = jnp.dot(x_blk, down_matrix, preferred_element_type=jnp.float32).astype(jnp.bfloat16)
        raised_output = jnp.dot(low, up_matrix, preferred_element_type=jnp.float32)
        low_rank_gradient = (adapter_scale * jnp.dot(output_gradient_block, up_matrix.T, preferred_element_type=jnp.float32)).astype(jnp.bfloat16)
        back = jnp.dot(low_rank_gradient, down_matrix.T, preferred_element_type=jnp.float32)
        term_down = jnp.dot(x_blk.T, low_rank_gradient, preferred_element_type=jnp.float32).astype(jnp.bfloat16)
        term_up = jnp.dot(low.T, output_gradient_block, preferred_element_type=jnp.float32).astype(jnp.bfloat16)
        term_down = lax.optimization_barrier(term_down).astype(jnp.float32)
        term_up = lax.optimization_barrier(term_up).astype(jnp.float32)
        acc_down = acc_down.at[row_position].add(term_down)
        acc_up = acc_up.at[row_position].add(term_up)
        return (acc_down, acc_up), (raised_output, back)

    start = (jnp.zeros((ADAPTER_TOTAL, MODEL_WIDTH, ADAPTER_RANK), jnp.float32), jnp.zeros((ADAPTER_TOTAL, ADAPTER_RANK, VALUE_WIDTH), jnp.float32))
    (acc_down, acc_up), (raised_output, back) = lax.scan(step, start, (x_blocks, dy_blocks, spot))
    frozen_output = jnp.dot(inputs, frozen_value_weight, preferred_element_type=jnp.float32)
    values = (frozen_output + adapter_scale * raised_output.reshape(ROW_TOTAL, VALUE_WIDTH)).astype(jnp.bfloat16)
    grad_base = jnp.dot(value_gradient, frozen_value_weight.T, preferred_element_type=jnp.float32)
    grad_inputs = (grad_base + back.reshape(ROW_TOTAL, MODEL_WIDTH)).astype(jnp.bfloat16)
    return values, grad_inputs, acc_down.astype(jnp.bfloat16), acc_up.astype(jnp.bfloat16)
```

```python
import jax
import jax.numpy as jnp
from jax import lax
from jax.sharding import PartitionSpec as P

BLOCK = 128


adapter_scale = 0.5


def exchange(pieces):
    return lax.all_to_all(pieces, "dp", split_axis=0, concat_axis=0, tiled=True)


def cut(mats, parts):
    m, rank, width = mats.shape
    rows = rank // parts
    return mats.reshape(m, parts, rows * width).swapaxes(0, 1)


def join(pieces, width):
    parts, m, size = pieces.shape
    return pieces.swapaxes(0, 1).reshape(m, parts * (size // width), width)


def on_device(
    inputs,
    frozen_value_weight,
    adapter_down_weight,
    adapter_up_weight,
    adapter_per_block,
    adapter_storage_index,
    value_gradient,
):
    n = lax.axis_size("dp")
    nblocks = adapter_per_block.shape[0]
    kept = adapter_down_weight.shape[0]
    total = adapter_storage_index.shape[0]
    rows = inputs.shape[0]
    feat = inputs.shape[1]
    columns = value_gradient.shape[1]
    f32, bf16 = jnp.float32, jnp.bfloat16

    up_table = exchange(cut(adapter_up_weight, n)).reshape(total, -1)
    down_table = exchange(cut(adapter_down_weight.swapaxes(1, 2), n)).reshape(total, -1)

    spot = adapter_storage_index[adapter_per_block]
    spots = lax.all_gather(spot, "dp", axis=0, tiled=True)
    pick = (spots[:, None] == jnp.arange(total, dtype=jnp.int32)[None, :]).astype(bf16)

    def fetch(table, width):
        chosen = jnp.dot(pick, table, preferred_element_type=f32).astype(bf16)
        return join(exchange(chosen.reshape(n, nblocks, -1)), width)

    def give(terms, width):
        pieces = exchange(cut(terms, n)).reshape(n * nblocks, -1)
        sums = lax.dot_general(
            pick, pieces, (((0,), (0,)), ((), ())), preferred_element_type=f32
        ).astype(bf16)
        return join(exchange(sums.reshape(n, kept, -1)), width)

    block_up = fetch(up_table, columns)
    block_down = fetch(down_table, feat)

    x_blocks = inputs.reshape(nblocks, BLOCK, feat)
    dy_blocks = value_gradient.reshape(nblocks, BLOCK, columns)

    partial_low_gradient = adapter_scale * jnp.einsum(
        "bnk,brk->bnr", dy_blocks, block_up, preferred_element_type=f32
    )
    low_rank_gradient = lax.psum(partial_low_gradient, "tensor").astype(bf16)
    term_down = jnp.einsum(
        "bnd,bnr->brd", x_blocks, low_rank_gradient, preferred_element_type=f32
    ).astype(bf16)
    grad_down = give(term_down, feat).swapaxes(1, 2)

    partial_base = jnp.dot(inputs, frozen_value_weight, preferred_element_type=f32)
    frozen_output = lax.psum_scatter(partial_base, "tensor", scatter_dimension=1, tiled=True)
    low_part = jnp.einsum("bnd,brd->bnr", x_blocks, block_down, preferred_element_type=f32)
    low = lax.psum(low_part, "tensor").astype(bf16)
    term_up = jnp.einsum("bnr,bnk->brk", low, dy_blocks, preferred_element_type=f32).astype(bf16)
    grad_up = give(term_up, columns)

    raised_output = jnp.einsum("bnr,brk->bnk", low, block_up, preferred_element_type=f32)
    values = (frozen_output + adapter_scale * raised_output.reshape(rows, columns)).astype(bf16)
    grad_base = lax.dot_general(
        lax.all_gather(value_gradient, "tensor", axis=1, tiled=True),
        frozen_value_weight,
        (((1,), (1,)), ((), ())),
        preferred_element_type=f32,
    )
    back = jnp.einsum("bnr,brd->bnd", low_rank_gradient, block_down, preferred_element_type=f32)
    grad_inputs = (grad_base + back.reshape(rows, feat)).astype(bf16)
    return (values, grad_inputs, grad_down, grad_up)


def solution(mesh):
    return jax.shard_map(
        on_device,
        mesh=mesh,
        in_specs=(
            P("dp", "tensor"),
            P("tensor", None),
            P("dp", "tensor", None),
            P("dp", None, "tensor"),
            P("dp"),
            P(),
            P("dp", "tensor"),
        ),
        out_specs=(
            P("dp", "tensor"),
            P("dp", "tensor"),
            P("dp", "tensor", None),
            P("dp", None, "tensor"),
        ),
        check_vma=False,
    )
```

```python
import functools

import jax
import jax.numpy as jnp
from jax import lax
from jax.experimental import pallas as pl
from jax.experimental.pallas import tpu as pltpu
from jax.sharding import PartitionSpec as P

BLOCK = 128
MESH = pl.DeviceIdType.MESH
f32, bf16, i32 = jnp.float32, jnp.bfloat16, jnp.int32
adapter_scale = 0.5

NX, NY, NC, NZ = 4, 4, 2, 8
DP = NX * NY * NC


def nt(a, b):
    return lax.dot_general(a, b, (((1,), (1,)), ((), ())), preferred_element_type=f32)


def tn(a, b):
    return lax.dot_general(a, b, (((0,), (0,)), ((), ())), preferred_element_type=f32)


def nn(a, b):
    return jnp.dot(a, b, preferred_element_type=f32)


class Sems:
    def __init__(self, ref):
        self.ref, self.used = ref, 0

    def take(self):
        self.used += 1
        return self.ref.at[self.used - 1]


def kernel(
    apb,
    asi,
    x_hbm,
    w_hbm,
    d_hbm,
    u_hbm,
    dy_hbm,
    values_out,
    gi_out,
    gd_out,
    gu_out,
    sem_ref,
    xv,
    wv,
    uv,
    dyv,
    spot,
    spot_in,
    spot_all,
    spot_s,
    lu_s,
    ru,
    u_t,
    fu,
    ub,
    d1a1,
    d1a2,
    d1b1,
    d1b2,
    table,
    chosen,
    d2_t,
    bd,
    yv,
    rs_send,
    rs_recv,
    dyall,
    ar_part,
    ar_in,
    ar_mid,
    glt,
    lowt,
    lmat,
    term,
    g2_t,
    pieces,
    sums,
    g1_t,
    tu,
    su,
    ug_t,
    gu,
    guv,
    giv,
    valv,
):
    i = lax.axis_index("dp")
    z = lax.axis_index("tensor")
    c = lax.rem(i, NC)
    y = lax.rem(lax.div(i, NC), NY)
    x = lax.div(i, NC * NY)
    sems = Sems(sem_ref)

    def dev(xx=x, yy=y, cc=c, zz=z):
        return ((xx * NY + yy) * NC + cc, zz)

    def turn(v, d, n):
        return lax.rem(v + d, n)

    def remote(src, dst, device):
        copy = pltpu.make_async_remote_copy(
            src_ref=src,
            dst_ref=dst,
            send_sem=sems.take(),
            recv_sem=sems.take(),
            device_id=device,
            device_id_type=MESH,
        )
        copy.start()
        return copy

    def local(src, dst):
        copy = pltpu.make_async_copy(src, dst, sems.take())
        copy.start()
        return copy

    def wait(copies):
        for copy in copies:
            copy.wait()

    def step(axis, src, dst):
        own, size = {"x": (x, NX), "y": (y, NY), "c": (c, NC)}[axis]
        key = {"x": "xx", "y": "yy", "c": "cc"}[axis]
        copies = []
        for d in (1, 3, 2) if size == 4 else (1,):
            to = turn(own, d, size)
            copies.append(remote(src(to), dst(own), dev(**{key: to})))
        copies.append(local(src(own), dst(own)))
        return copies

    class Exchange:
        def __init__(self, slots, mid, out):
            self.slots, self.mid, self.out = slots, mid, out

        def first(self):
            s, m = self.slots, self.mid
            self.copies = step("x", lambda t: s.at[t, :, :, 0], lambda o: m.at[0, o]) + step(
                "y", lambda t: s.at[:, t, :, 1], lambda o: m.at[1, :, o]
            )

        def second(self):
            wait(self.copies)
            m = self.mid
            self.copies = step("y", lambda t: m.at[0, :, t], lambda o: m.at[2, :, o]) + step(
                "x", lambda t: m.at[1, t], lambda o: m.at[3, o]
            )

        def third(self):
            wait(self.copies)
            m, out = self.mid, self.out
            self.copies = step("c", lambda t: m.at[2, :, :, t], lambda o: out.at[:, :, o, 0]) + step(
                "c", lambda t: m.at[3, :, :, t], lambda o: out.at[:, :, o, 1]
            )

        def finish(self):
            wait(self.copies)

    def lanes(k, width):
        return pl.ds(pl.multiple_of(k * width, width), width)

    class Down:
        def first(self):
            self.copies = step(
                "x",
                lambda t: d_hbm.at[pl.ds(0, 8), :, :, :, lanes(t, 256)],
                lambda o: d1a1.at[o],
            ) + step("y", lambda t: d_hbm.at[pl.ds(8, 8), t], lambda o: d1b1.at[o])

        def second(self):
            wait(self.copies)
            self.copies = step("y", lambda t: d1a1.at[:, :, t], lambda o: d1a2.at[:, o]) + step(
                "x", lambda t: d1b1.at[:, :, :, :, lanes(t, 256)], lambda o: d1b2.at[o]
            )

        def third(self):
            wait(self.copies)
            self.copies = step("c", lambda t: d1a2.at[:, :, :, t], lambda o: table.at[o, 0]) + step(
                "c", lambda t: d1b2.at[:, :, :, t], lambda o: table.at[o, 1]
            )

        def finish(self):
            wait(self.copies)

    class Gather:
        def slot(self, k):
            return dyall.at[lax.div(k, 2), :, lanes(lax.rem(k, 2), BLOCK)]

        def start(self, s):
            self.copies = []
            for d, last in ((1, 4), (NZ - 1, 3)):
                if s < last:
                    k = turn(z, (NZ - d) * s, NZ)
                    src = dyv if s == 0 else self.slot(k)
                    self.copies.append(remote(src, self.slot(k), dev(zz=turn(z, d, NZ))))
            if s == 0:
                self.own = local(dyv, self.slot(z))

        def finish(self, s):
            wait(self.copies)
            if s == 0:
                self.own.wait()

    class Scatter:
        def start(self, s):
            if s:
                wait(self.copies)
            self.copies = []
            for way, (d, last) in enumerate(((1, 4), (NZ - 1, 3))):
                if s < last:
                    own = yv[turn(z, d * (last - s), NZ)]
                    if s:
                        own = own + rs_recv[way, s - 1].astype(f32)
                    rs_send[way, s] = own.astype(bf16)
                    self.copies.append(
                        remote(rs_send.at[way, s], rs_recv.at[way, s], dev(zz=turn(z, d, NZ)))
                    )

        def finish(self):
            wait(self.copies)

    class Reduce:
        def __init__(self, k, out, scale):
            self.k, self.out, self.scale = k, out, scale

        def first(self):
            k = self.k
            self.copies = [
                remote(
                    ar_part.at[k, turn(z, d, NZ)],
                    ar_in.at[k, d - 1],
                    dev(zz=turn(z, d, NZ)),
                )
                for d in range(1, NZ)
            ]

        def second(self):
            k = self.k
            wait(self.copies)
            total = ar_part[k, z]
            for d in range(1, NZ):
                total = total + ar_in[k, d - 1]
            ar_mid[k] = (total * self.scale).astype(bf16)
            self.copies = [
                remote(ar_mid.at[k], self.out.at[z], dev(zz=turn(z, d, NZ))) for d in range(1, NZ)
            ] + [local(ar_mid.at[k], self.out.at[z])]

        def finish(self):
            wait(self.copies)

    barrier = pltpu.get_barrier_semaphore()
    peers = [dev(xx=turn(x, d, NX)) for d in range(1, NX)]
    peers += [dev(yy=turn(y, d, NY)) for d in range(1, NY)]
    peers += [dev(cc=turn(c, 1, NC))]
    peers += [dev(zz=turn(z, d, NZ)) for d in range(1, NZ)]
    for device in peers:
        pl.semaphore_signal(barrier, inc=1, device_id=device, device_id_type=MESH)
    load_dy = local(dy_hbm, dyv)
    load_u = local(u_hbm, uv)
    load_x = local(x_hbm, xv)
    load_w = local(w_hbm, wv)

    lane = lax.broadcasted_iota(i32, (8, 256), 1)
    mine = jnp.zeros((8, 256), i32)
    for b in range(8):
        mine = jnp.where(lane == i * 8 + b, asi[apb[b]], mine)
    spot[0] = mine
    pl.semaphore_wait(barrier, len(peers))

    down = Down()
    gather = Gather()
    scatter = Scatter()

    axes = (("xx", x, NX), ("yy", y, NY), ("cc", c, NC))
    for k, (key, own, size) in enumerate(axes):
        copies = [
            remote(spot.at[k], spot_in.at[3 * k + d - 1], dev(**{key: turn(own, d, size)}))
            for d in range(1, size)
        ]
        if k == 0:
            down.first()
            load_dy.wait()
            gather.start(0)
        wait(copies)
        total = spot[k]
        for d in range(1, size):
            total = total + spot_in[3 * k + d - 1]
        if k < 2:
            spot[k + 1] = total
        else:
            spot_all[...] = total
    local(spot_all, spot_s).wait()

    load_u.wait()

    def reply(k, _):
        found = jnp.int32(0)
        for b in range(8):
            s = spot_s[0, k * 8 + b]
            hit = lax.shift_right_logical(s, 4) == i
            found = jnp.where(hit, lax.bitwise_and(s, 15) + 1, found)
        lu_s[k] = found - 1
        chunk = uv[jnp.maximum(found - 1, 0)]
        ru[lax.div(k, 8), lax.rem(lax.div(k, 2), 4), lax.rem(k, 2)] = chunk
        return 0

    lax.fori_loop(0, DP, reply, 0)
    up = Exchange(ru, u_t, fu)
    up.first()

    load_x.wait()
    load_w.wait()

    def base(n, _):
        part = nn(xv[...], wv[:, lanes(n, 256)])
        yv[2 * n] = part[:, :BLOCK]
        yv[2 * n + 1] = part[:, BLOCK:]
        return 0

    lax.fori_loop(0, 4, base, 0)

    gather.finish(0)
    gather.start(1)
    down.second()
    up.second()
    gather.finish(1)
    gather.start(2)
    up.third()
    up.finish()

    for b in range(8):
        k = lax.shift_right_logical(spot_s[0, i * 8 + b], 4)
        chunk = fu[
            lax.shift_right_logical(k, 3),
            lax.bitwise_and(lax.shift_right_logical(k, 1), 3),
            lax.bitwise_and(k, 1),
        ]
        ub[b] = chunk.reshape(64, BLOCK)
    for b in range(8):
        ar_part[0, b] = nt(ub[b], dyv[b * BLOCK : (b + 1) * BLOCK])
    grad_low = Reduce(0, glt, adapter_scale)
    grad_low.first()

    gather.finish(2)
    gather.start(3)
    grad_low.second()
    down.third()
    down.finish()

    def choose(k, _):
        for b in range(8):
            s = spot_s[0, k * 8 + b]
            piece = table[
                lax.bitwise_and(lax.shift_right_logical(s, 4), 1),
                lax.bitwise_and(lax.shift_right_logical(s, 3), 1),
                lax.shift_right_logical(s, 7),
                lax.bitwise_and(lax.shift_right_logical(s, 5), 3),
                lax.bitwise_and(s, 7),
            ]
            chosen[lax.div(k, 8), lax.rem(lax.div(k, 2), 4), lax.rem(k, 2), b // 4, b % 4] = piece
        return 0

    lax.fori_loop(0, DP, choose, 0)
    fetch = Exchange(chosen, d2_t, bd)
    fetch.first()

    grad_low.finish()
    row = lax.broadcasted_iota(i32, (512, 64), 0)
    col = lax.broadcasted_iota(i32, (512, 64), 1)
    for b in range(8):
        spread = (row == col * 8 + b).astype(f32).astype(bf16)
        lmat[:, b * BLOCK : (b + 1) * BLOCK] = nn(spread, glt[b]).astype(bf16)

    def terms(n, _):
        part = nn(lmat[...], xv[:, lanes(n, 256)])
        term[:, :, :, :, :, lanes(n, 256)] = part.reshape(4, 4, 2, 2, 8, 256).astype(bf16)
        return 0

    lax.fori_loop(0, 4, terms, 0)
    give = Exchange(term, g2_t, pieces)
    give.first()

    fetch.second()
    gather.finish(3)
    scatter.start(0)
    give.second()
    fetch.third()
    fetch.finish()

    for b in range(8):
        part = jnp.zeros((64, BLOCK), f32)
        for q in range(4):
            mat = bd[q, :, :, b // 4, b % 4].reshape(64, 256)
            part = part + nt(mat, xv[b * BLOCK : (b + 1) * BLOCK, q * 256 : (q + 1) * 256])
        ar_part[1, b] = part
    low = Reduce(1, lowt, 1.0)
    low.first()
    scatter.start(1)
    give.third()
    give.finish()

    pick = (lax.broadcasted_iota(i32, (512, 256), 0) == spot_all[0:1, :]).astype(f32).astype(bf16)

    def add(n, _):
        for h in range(2):
            mat = pieces[:, :, :, h, :, lanes(n, 256)].reshape(256, 256)
            part = nn(pick, mat).astype(bf16)
            sums[:, :, :, h, :, lanes(n, 256)] = part.reshape(4, 4, 2, 16, 256)
        return 0

    lax.fori_loop(0, 4, add, 0)
    keep = Exchange(sums, g1_t, gd_out)
    keep.first()

    low.second()
    scatter.start(2)
    low.finish()
    for b in range(8):
        tu[b] = nn(lowt[b], dyv[b * BLOCK : (b + 1) * BLOCK]).astype(bf16).reshape(2, 32, BLOCK)

    def send_up(k, _):
        found = jnp.int32(0)
        for b in range(8):
            hit = lax.shift_right_logical(spot_s[0, i * 8 + b], 4) == k
            found = jnp.where(hit, b + 1, found)
        chunk = tu[jnp.maximum(found - 1, 0)].astype(f32)
        chunk = jnp.where(found > 0, chunk, 0.0)
        su[lax.div(k, 8), lax.rem(lax.div(k, 2), 4), lax.rem(k, 2)] = chunk.astype(bf16)
        return 0

    lax.fori_loop(0, DP, send_up, 0)
    give_up = Exchange(su, ug_t, gu)
    give_up.first()

    def backward(n, _):
        part = jnp.zeros((1024, 256), f32)
        for k in range(4):
            part = part + nt(dyall[k], wv[lanes(n, 256), k * 256 : (k + 1) * 256])
        for b in range(8):
            rows = slice(b * BLOCK, (b + 1) * BLOCK)
            mat = bd[n, :, :, b // 4, b % 4].reshape(64, 256)
            giv[rows, lanes(n, 256)] = (part[rows] + tn(glt[b], mat)).astype(bf16)
        return 0

    lax.fori_loop(0, 4, backward, 0)
    store_gi = local(giv, gi_out)
    scatter.start(3)
    keep.second()
    give_up.second()
    give_up.third()
    give_up.finish()

    def add_up(k, _):
        def one(j, total):
            chunk = gu[lax.div(j, 8), lax.rem(lax.div(j, 2), 4), lax.rem(j, 2)].astype(f32)
            return total + jnp.where(lu_s[j] == k, chunk, 0.0)

        total = lax.fori_loop(0, DP, one, jnp.zeros((2, 32, BLOCK), f32))
        guv[k] = total.astype(bf16)
        return 0

    lax.fori_loop(0, 16, add_up, 0)
    store_gu = local(guv, gu_out)
    scatter.finish()
    for b in range(8):
        rows = slice(b * BLOCK, (b + 1) * BLOCK)
        frozen = yv[z, rows] + rs_recv[0, 3, rows].astype(f32) + rs_recv[1, 2, rows].astype(f32)
        valv[rows] = (frozen + adapter_scale * tn(lowt[b], ub[b])).astype(bf16)
    store_values = local(valv, values_out)
    keep.third()
    keep.finish()
    wait([store_gi, store_gu, store_values])
    assert sems.used <= sem_ref.shape[0], sems.used


def on_device(inputs, frozen, down, up, apb, asi, dy):
    any_ = pl.BlockSpec(memory_space=pl.ANY)
    smem = pl.BlockSpec(memory_space=pltpu.SMEM)

    def v(*shape, dtype=bf16):
        return pltpu.VMEM(shape, dtype)

    values, grad_inputs, gd, gu = pl.pallas_call(
        kernel,
        out_shape=(
            jax.ShapeDtypeStruct((1024, 128), bf16),
            jax.ShapeDtypeStruct((1024, 1024), bf16),
            jax.ShapeDtypeStruct((4, 4, 2, 2, 16, 1024), bf16),
            jax.ShapeDtypeStruct((16, 2, 32, 128), bf16),
        ),
        in_specs=[smem, smem, any_, any_, any_, any_, any_],
        out_specs=(any_,) * 4,
        scratch_shapes=[
            pltpu.SemaphoreType.DMA((340,)),
            v(1024, 1024),
            v(1024, 1024),
            v(16, 2, 32, 128),
            v(1024, 128),
            v(3, 8, 256, dtype=i32),
            v(7, 8, 256, dtype=i32),
            v(8, 256, dtype=i32),
            pltpu.SMEM((8, 256), i32),
            pltpu.SMEM((32,), i32),
            v(4, 4, 2, 2, 32, 128),
            v(4, 4, 4, 2, 32, 128),
            v(4, 4, 2, 2, 32, 128),
            v(8, 64, 128),
            v(4, 8, 4, 2, 8, 256),
            v(4, 4, 8, 2, 8, 256),
            v(4, 8, 2, 8, 1024),
            v(4, 4, 8, 2, 8, 256),
            v(2, 2, 4, 4, 8, 8, 256),
            v(4, 4, 2, 2, 4, 8, 256),
            v(4, 4, 4, 2, 4, 8, 256),
            v(4, 4, 2, 2, 4, 8, 256),
            v(8, 1024, 128, dtype=f32),
            v(2, 4, 1024, 128),
            v(2, 4, 1024, 128),
            v(4, 1024, 256),
            v(2, 8, 64, 128, dtype=f32),
            v(2, 7, 64, 128, dtype=f32),
            v(2, 64, 128),
            v(8, 64, 128),
            v(8, 64, 128),
            v(512, 1024),
            v(4, 4, 2, 2, 8, 1024),
            v(4, 4, 4, 2, 8, 1024),
            v(4, 4, 2, 2, 8, 1024),
            v(4, 4, 2, 2, 16, 1024),
            v(4, 4, 4, 2, 16, 1024),
            v(8, 2, 32, 128),
            v(4, 4, 2, 2, 32, 128),
            v(4, 4, 4, 2, 32, 128),
            v(4, 4, 2, 2, 32, 128),
            v(16, 2, 32, 128),
            v(1024, 1024),
            v(1024, 128),
        ],
        compiler_params=pltpu.CompilerParams(
            collective_id=0, has_side_effects=True, vmem_limit_bytes=60 * 2**20
        ),
    )(
        apb,
        asi,
        inputs,
        frozen,
        down.swapaxes(1, 2).reshape(16, 4, 2, 8, 1024),
        up.reshape(16, 2, 32, 128),
        dy,
    )
    grad_down = gd.reshape(64, 16, 1024).transpose(1, 2, 0)
    return values, grad_inputs, grad_down, gu.reshape(16, 64, 128)


def solution(mesh):
    return jax.shard_map(
        on_device,
        mesh=mesh,
        in_specs=(
            P("dp", "tensor"),
            P("tensor", None),
            P("dp", "tensor", None),
            P("dp", None, "tensor"),
            P("dp"),
            P(),
            P("dp", "tensor"),
        ),
        out_specs=(
            P("dp", "tensor"),
            P("dp", "tensor"),
            P("dp", "tensor", None),
            P("dp", None, "tensor"),
        ),
        check_vma=False,
    )
```

```python
import functools

import jax
import jax.numpy as jnp
from jax import lax
from jax.experimental import pallas as pl
from jax.experimental.pallas import tpu as pltpu
from jax.sharding import PartitionSpec as P

BLOCK = 128
MESH = pl.DeviceIdType.MESH
f32, bf16, i32 = jnp.float32, jnp.bfloat16, jnp.int32
adapter_scale = 0.5

NX, NY, NC, NZ = 4, 4, 2, 8
DP = NX * NY * NC


def nt(a, b):
    return lax.dot_general(a, b, (((1,), (1,)), ((), ())), preferred_element_type=f32)


def tn(a, b):
    return lax.dot_general(a, b, (((0,), (0,)), ((), ())), preferred_element_type=f32)


def nn(a, b):
    return jnp.dot(a, b, preferred_element_type=f32)


class Sems:
    def __init__(self, ref):
        self.ref, self.used = ref, 0

    def take(self):
        self.used += 1
        return self.ref.at[self.used - 1]


def kernel(
    apb,
    asi,
    x_hbm,
    w_hbm,
    d_hbm,
    u_hbm,
    dy_hbm,
    values_out,
    gi_out,
    gd_out,
    gu_out,
    sem_ref,
    xv,
    wv,
    uv,
    dyv,
    spot,
    spot_in,
    spot_all,
    spot_s,
    lu_s,
    ru,
    u_t,
    fu,
    ub,
    d1a1,
    d1a2,
    d1b1,
    d1b2,
    table,
    chosen,
    d2_t,
    bd,
    yv,
    rs_send,
    rs_recv,
    dyall,
    ar_part,
    ar_in,
    ar_mid,
    glt,
    lowt,
    lmat,
    term,
    g2_t,
    pieces,
    sums,
    g1_t,
    tu,
    su,
    ug_t,
    gu,
    guv,
    giv,
    valv,
):
    i = lax.axis_index("dp")
    z = lax.axis_index("tensor")
    c = lax.rem(i, NC)
    y = lax.rem(lax.div(i, NC), NY)
    x = lax.div(i, NC * NY)
    sems = Sems(sem_ref)

    def dev(xx=x, yy=y, cc=c, zz=z):
        return ((xx * NY + yy) * NC + cc, zz)

    def turn(v, d, n):
        return lax.rem(v + d, n)

    def remote(src, dst, device):
        copy = pltpu.make_async_remote_copy(
            src_ref=src,
            dst_ref=dst,
            send_sem=sems.take(),
            recv_sem=sems.take(),
            device_id=device,
            device_id_type=MESH,
        )
        copy.start()
        return copy

    def local(src, dst):
        copy = pltpu.make_async_copy(src, dst, sems.take())
        copy.start()
        return copy

    def wait(copies):
        for copy in copies:
            copy.wait()

    def step(axis, src, dst):
        own, size = {"x": (x, NX), "y": (y, NY), "c": (c, NC)}[axis]
        key = {"x": "xx", "y": "yy", "c": "cc"}[axis]
        copies = []
        for d in (1, 3, 2) if size == 4 else (1,):
            to = turn(own, d, size)
            copies.append(remote(src(to), dst(own), dev(**{key: to})))
        copies.append(local(src(own), dst(own)))
        return copies

    class Exchange:
        def __init__(self, slots, mid, out):
            self.slots, self.mid, self.out = slots, mid, out

        def first(self):
            s, m = self.slots, self.mid
            self.copies = step("x", lambda t: s.at[t, :, :, 0], lambda o: m.at[0, o]) + step(
                "y", lambda t: s.at[:, t, :, 1], lambda o: m.at[1, :, o]
            )

        def second(self):
            wait(self.copies)
            m = self.mid
            self.copies = step("y", lambda t: m.at[0, :, t], lambda o: m.at[2, :, o]) + step(
                "x", lambda t: m.at[1, t], lambda o: m.at[3, o]
            )

        def third(self):
            wait(self.copies)
            m, out = self.mid, self.out
            self.copies = step("c", lambda t: m.at[2, :, :, t], lambda o: out.at[:, :, o, 0]) + step(
                "c", lambda t: m.at[3, :, :, t], lambda o: out.at[:, :, o, 1]
            )

        def finish(self):
            wait(self.copies)

    def lanes(k, width):
        return pl.ds(pl.multiple_of(k * width, width), width)

    class Down:
        def first(self):
            self.copies = step(
                "x",
                lambda t: d_hbm.at[pl.ds(0, 8), :, :, :, lanes(t, 256)],
                lambda o: d1a1.at[o],
            ) + step("y", lambda t: d_hbm.at[pl.ds(8, 8), t], lambda o: d1b1.at[o])

        def second(self):
            wait(self.copies)
            self.copies = step("y", lambda t: d1a1.at[:, :, t], lambda o: d1a2.at[:, o]) + step(
                "x", lambda t: d1b1.at[:, :, :, :, lanes(t, 256)], lambda o: d1b2.at[o]
            )

        def third(self):
            wait(self.copies)
            self.copies = step("c", lambda t: d1a2.at[:, :, :, t], lambda o: table.at[o, 0]) + step(
                "c", lambda t: d1b2.at[:, :, :, t], lambda o: table.at[o, 1]
            )

        def finish(self):
            wait(self.copies)

    class Gather:
        def slot(self, k):
            return dyall.at[lax.div(k, 2), :, lanes(lax.rem(k, 2), BLOCK)]

        def start(self, s):
            self.copies = []
            for d, last in ((1, 4), (NZ - 1, 3)):
                if s < last:
                    k = turn(z, (NZ - d) * s, NZ)
                    src = dyv if s == 0 else self.slot(k)
                    self.copies.append(remote(src, self.slot(k), dev(zz=turn(z, d, NZ))))
            if s == 0:
                self.own = local(dyv, self.slot(z))

        def finish(self, s):
            wait(self.copies)
            if s == 0:
                self.own.wait()

    class Scatter:
        def start(self, s):
            if s:
                wait(self.copies)
            self.copies = []
            for way, (d, last) in enumerate(((1, 4), (NZ - 1, 3))):
                if s < last:
                    own = yv[turn(z, d * (last - s), NZ)]
                    if s:
                        own = own + rs_recv[way, s - 1].astype(f32)
                    rs_send[way, s] = own.astype(bf16)
                    self.copies.append(
                        remote(rs_send.at[way, s], rs_recv.at[way, s], dev(zz=turn(z, d, NZ)))
                    )

        def finish(self):
            wait(self.copies)

    class Reduce:
        def __init__(self, k, out, scale):
            self.k, self.out, self.scale = k, out, scale

        def first(self):
            k = self.k
            self.copies = [
                remote(
                    ar_part.at[k, turn(z, d, NZ)],
                    ar_in.at[k, d - 1],
                    dev(zz=turn(z, d, NZ)),
                )
                for d in range(1, NZ)
            ]

        def second(self):
            k = self.k
            wait(self.copies)
            total = ar_part[k, z]
            for d in range(1, NZ):
                total = total + ar_in[k, d - 1]
            ar_mid[k] = (total * self.scale).astype(bf16)
            self.copies = [
                remote(ar_mid.at[k], self.out.at[z], dev(zz=turn(z, d, NZ))) for d in range(1, NZ)
            ] + [local(ar_mid.at[k], self.out.at[z])]

        def finish(self):
            wait(self.copies)

    barrier = pltpu.get_barrier_semaphore()
    peers = [dev(xx=turn(x, d, NX)) for d in range(1, NX)]
    peers += [dev(yy=turn(y, d, NY)) for d in range(1, NY)]
    peers += [dev(cc=turn(c, 1, NC))]
    peers += [dev(zz=turn(z, d, NZ)) for d in range(1, NZ)]
    for device in peers:
        pl.semaphore_signal(barrier, inc=1, device_id=device, device_id_type=MESH)
    load_dy = local(dy_hbm, dyv)
    load_u = local(u_hbm, uv)
    load_x = local(x_hbm, xv)
    load_w = local(w_hbm, wv)

    lane = lax.broadcasted_iota(i32, (8, 256), 1)
    mine = jnp.zeros((8, 256), i32)
    for b in range(8):
        mine = jnp.where(lane == i * 8 + b, asi[apb[b]], mine)
    spot[0] = mine
    pl.semaphore_wait(barrier, len(peers))

    down = Down()
    gather = Gather()
    scatter = Scatter()

    axes = (("xx", x, NX), ("yy", y, NY), ("cc", c, NC))
    for k, (key, own, size) in enumerate(axes):
        copies = [
            remote(spot.at[k], spot_in.at[3 * k + d - 1], dev(**{key: turn(own, d, size)}))
            for d in range(1, size)
        ]
        if k == 0:
            down.first()
            load_dy.wait()
            gather.start(0)
        wait(copies)
        total = spot[k]
        for d in range(1, size):
            total = total + spot_in[3 * k + d - 1]
        if k < 2:
            spot[k + 1] = total
        else:
            spot_all[...] = total
    local(spot_all, spot_s).wait()

    load_u.wait()

    def reply(k, _):
        found = jnp.int32(0)
        for b in range(8):
            s = spot_s[0, k * 8 + b]
            hit = lax.shift_right_logical(s, 4) == i
            found = jnp.where(hit, lax.bitwise_and(s, 15) + 1, found)
        lu_s[k] = found - 1
        chunk = uv[jnp.maximum(found - 1, 0)]
        ru[lax.div(k, 8), lax.rem(lax.div(k, 2), 4), lax.rem(k, 2)] = chunk
        return 0

    lax.fori_loop(0, DP, reply, 0)
    up = Exchange(ru, u_t, fu)
    up.first()
    down.second()
    gather.finish(0)
    gather.start(1)

    load_x.wait()
    load_w.wait()

    def base(n, _):
        part = nn(xv[...], wv[:, lanes(n, 256)])
        yv[2 * n] = part[:, :BLOCK]
        yv[2 * n + 1] = part[:, BLOCK:]
        return 0

    lax.fori_loop(0, 4, base, 0)
    up.second()
    gather.finish(1)
    gather.start(2)
    up.third()
    up.finish()

    for b in range(8):
        k = lax.shift_right_logical(spot_s[0, i * 8 + b], 4)
        chunk = fu[
            lax.shift_right_logical(k, 3),
            lax.bitwise_and(lax.shift_right_logical(k, 1), 3),
            lax.bitwise_and(k, 1),
        ]
        ub[b] = chunk.reshape(64, BLOCK)
    for b in range(8):
        ar_part[0, b] = nt(ub[b], dyv[b * BLOCK : (b + 1) * BLOCK])
    grad_low = Reduce(0, glt, adapter_scale)
    grad_low.first()
    down.third()
    grad_low.second()
    down.finish()

    def choose(k, _):
        for b in range(8):
            s = spot_s[0, k * 8 + b]
            piece = table[
                lax.bitwise_and(lax.shift_right_logical(s, 4), 1),
                lax.bitwise_and(lax.shift_right_logical(s, 3), 1),
                lax.shift_right_logical(s, 7),
                lax.bitwise_and(lax.shift_right_logical(s, 5), 3),
                lax.bitwise_and(s, 7),
            ]
            chosen[lax.div(k, 8), lax.rem(lax.div(k, 2), 4), lax.rem(k, 2), b // 4, b % 4] = piece
        return 0

    lax.fori_loop(0, DP, choose, 0)
    fetch = Exchange(chosen, d2_t, bd)
    fetch.first()

    grad_low.finish()
    row = lax.broadcasted_iota(i32, (512, 64), 0)
    col = lax.broadcasted_iota(i32, (512, 64), 1)
    for b in range(8):
        spread = (row == col * 8 + b).astype(f32).astype(bf16)
        lmat[:, b * BLOCK : (b + 1) * BLOCK] = nn(spread, glt[b]).astype(bf16)

    def terms(n, _):
        part = nn(lmat[...], xv[:, lanes(n, 256)])
        term[:, :, :, :, :, lanes(n, 256)] = part.reshape(4, 4, 2, 2, 8, 256).astype(bf16)
        return 0

    lax.fori_loop(0, 4, terms, 0)
    give = Exchange(term, g2_t, pieces)
    give.first()
    gather.finish(2)
    gather.start(3)
    fetch.second()
    pick = (lax.broadcasted_iota(i32, (512, 256), 0) == spot_all[0:1, :]).astype(f32).astype(bf16)
    give.second()
    fetch.third()
    gather.finish(3)
    scatter.start(0)
    fetch.finish()

    for b in range(8):
        part = jnp.zeros((64, BLOCK), f32)
        for q in range(4):
            mat = bd[q, :, :, b // 4, b % 4].reshape(64, 256)
            part = part + nt(mat, xv[b * BLOCK : (b + 1) * BLOCK, q * 256 : (q + 1) * 256])
        ar_part[1, b] = part
    low = Reduce(1, lowt, 1.0)
    low.first()
    give.third()
    give.finish()

    def add(n, _):
        for h in range(2):
            mat = pieces[:, :, :, h, :, lanes(n, 256)].reshape(256, 256)
            part = nn(pick, mat).astype(bf16)
            sums[:, :, :, h, :, lanes(n, 256)] = part.reshape(4, 4, 2, 16, 256)
        return 0

    lax.fori_loop(0, 4, add, 0)
    keep = Exchange(sums, g1_t, gd_out)
    keep.first()

    low.second()
    scatter.start(1)
    low.finish()
    for b in range(8):
        tu[b] = nn(lowt[b], dyv[b * BLOCK : (b + 1) * BLOCK]).astype(bf16).reshape(2, 32, BLOCK)

    def send_up(k, _):
        found = jnp.int32(0)
        for b in range(8):
            hit = lax.shift_right_logical(spot_s[0, i * 8 + b], 4) == k
            found = jnp.where(hit, b + 1, found)
        chunk = tu[jnp.maximum(found - 1, 0)].astype(f32)
        chunk = jnp.where(found > 0, chunk, 0.0)
        su[lax.div(k, 8), lax.rem(lax.div(k, 2), 4), lax.rem(k, 2)] = chunk.astype(bf16)
        return 0

    lax.fori_loop(0, DP, send_up, 0)
    give_up = Exchange(su, ug_t, gu)
    give_up.first()
    scatter.start(2)
    give_up.second()
    keep.second()

    def backward(n, _):
        part = jnp.zeros((1024, 256), f32)
        for k in range(4):
            part = part + nt(dyall[k], wv[lanes(n, 256), k * 256 : (k + 1) * 256])
        for b in range(8):
            rows = slice(b * BLOCK, (b + 1) * BLOCK)
            mat = bd[n, :, :, b // 4, b % 4].reshape(64, 256)
            giv[rows, lanes(n, 256)] = (part[rows] + tn(glt[b], mat)).astype(bf16)
        return 0

    lax.fori_loop(0, 4, backward, 0)
    store_gi = local(giv, gi_out)
    give_up.third()
    scatter.start(3)
    give_up.finish()

    def add_up(k, _):
        total = jnp.zeros((2, 32, BLOCK), f32)
        for j in range(DP):
            share = jnp.where(lu_s[j] == k, 1.0, 0.0).astype(f32)
            total = total + gu[j // 8, (j // 2) % 4, j % 2].astype(f32) * share
        guv[k] = total.astype(bf16)
        return 0

    lax.fori_loop(0, 16, add_up, 0)
    store_gu = local(guv, gu_out)
    scatter.finish()
    for b in range(8):
        rows = slice(b * BLOCK, (b + 1) * BLOCK)
        frozen = yv[z, rows] + rs_recv[0, 3, rows].astype(f32) + rs_recv[1, 2, rows].astype(f32)
        valv[rows] = (frozen + adapter_scale * tn(lowt[b], ub[b])).astype(bf16)
    store_values = local(valv, values_out)
    keep.third()
    keep.finish()
    wait([store_gi, store_gu, store_values])
    assert sems.used <= sem_ref.shape[0], sems.used


def on_device(inputs, frozen, down, up, apb, asi, dy):
    any_ = pl.BlockSpec(memory_space=pl.ANY)
    smem = pl.BlockSpec(memory_space=pltpu.SMEM)

    def v(*shape, dtype=bf16):
        return pltpu.VMEM(shape, dtype)

    values, grad_inputs, gd, gu = pl.pallas_call(
        kernel,
        out_shape=(
            jax.ShapeDtypeStruct((1024, 128), bf16),
            jax.ShapeDtypeStruct((1024, 1024), bf16),
            jax.ShapeDtypeStruct((4, 4, 2, 2, 16, 1024), bf16),
            jax.ShapeDtypeStruct((16, 2, 32, 128), bf16),
        ),
        in_specs=[smem, smem, any_, any_, any_, any_, any_],
        out_specs=(any_,) * 4,
        scratch_shapes=[
            pltpu.SemaphoreType.DMA((340,)),
            v(1024, 1024),
            v(1024, 1024),
            v(16, 2, 32, 128),
            v(1024, 128),
            v(3, 8, 256, dtype=i32),
            v(7, 8, 256, dtype=i32),
            v(8, 256, dtype=i32),
            pltpu.SMEM((8, 256), i32),
            pltpu.SMEM((32,), i32),
            v(4, 4, 2, 2, 32, 128),
            v(4, 4, 4, 2, 32, 128),
            v(4, 4, 2, 2, 32, 128),
            v(8, 64, 128),
            v(4, 8, 4, 2, 8, 256),
            v(4, 4, 8, 2, 8, 256),
            v(4, 8, 2, 8, 1024),
            v(4, 4, 8, 2, 8, 256),
            v(2, 2, 4, 4, 8, 8, 256),
            v(4, 4, 2, 2, 4, 8, 256),
            v(4, 4, 4, 2, 4, 8, 256),
            v(4, 4, 2, 2, 4, 8, 256),
            v(8, 1024, 128, dtype=f32),
            v(2, 4, 1024, 128),
            v(2, 4, 1024, 128),
            v(4, 1024, 256),
            v(2, 8, 64, 128, dtype=f32),
            v(2, 7, 64, 128, dtype=f32),
            v(2, 64, 128),
            v(8, 64, 128),
            v(8, 64, 128),
            v(512, 1024),
            v(4, 4, 2, 2, 8, 1024),
            v(4, 4, 4, 2, 8, 1024),
            v(4, 4, 2, 2, 8, 1024),
            v(4, 4, 2, 2, 16, 1024),
            v(4, 4, 4, 2, 16, 1024),
            v(8, 2, 32, 128),
            v(4, 4, 2, 2, 32, 128),
            v(4, 4, 4, 2, 32, 128),
            v(4, 4, 2, 2, 32, 128),
            v(16, 2, 32, 128),
            v(1024, 1024),
            v(1024, 128),
        ],
        compiler_params=pltpu.CompilerParams(
            collective_id=0, has_side_effects=True, vmem_limit_bytes=60 * 2**20
        ),
    )(
        apb,
        asi,
        inputs,
        frozen,
        down.swapaxes(1, 2).reshape(16, 4, 2, 8, 1024),
        up.reshape(16, 2, 32, 128),
        dy,
    )
    grad_down = gd.reshape(64, 16, 1024).transpose(1, 2, 0)
    return values, grad_inputs, grad_down, gu.reshape(16, 64, 128)


def solution(mesh):
    return jax.shard_map(
        on_device,
        mesh=mesh,
        in_specs=(
            P("dp", "tensor"),
            P("tensor", None),
            P("dp", "tensor", None),
            P("dp", None, "tensor"),
            P("dp"),
            P(),
            P("dp", "tensor"),
        ),
        out_specs=(
            P("dp", "tensor"),
            P("dp", "tensor"),
            P("dp", "tensor", None),
            P("dp", None, "tensor"),
        ),
        check_vma=False,
    )
```

```python
import functools

import jax
import jax.numpy as jnp
from jax import lax
from jax.experimental import pallas as pl
from jax.experimental.pallas import tpu as pltpu
from jax.sharding import PartitionSpec as P

BLOCK = 128
MESH = pl.DeviceIdType.MESH
f32, bf16, i32 = jnp.float32, jnp.bfloat16, jnp.int32
adapter_scale = 0.5

NX, NY, NC, NZ = 4, 4, 2, 8
DP = NX * NY * NC


def nt(a, b):
    return lax.dot_general(a, b, (((1,), (1,)), ((), ())), preferred_element_type=f32)


def tn(a, b):
    return lax.dot_general(a, b, (((0,), (0,)), ((), ())), preferred_element_type=f32)


def nn(a, b):
    return jnp.dot(a, b, preferred_element_type=f32)


class Sems:
    def __init__(self, ref):
        self.ref, self.used = ref, 0

    def take(self):
        self.used += 1
        return self.ref.at[self.used - 1]


def kernel(
    apb,
    asi,
    x_hbm,
    w_hbm,
    d_hbm,
    u_hbm,
    dy_hbm,
    values_out,
    gi_out,
    gd_out,
    gu_out,
    sem_ref,
    xv,
    wv,
    uv,
    dyv,
    spot,
    spot_in,
    spot_all,
    spot_s,
    lu_s,
    ru,
    u_t,
    fu,
    ub,
    d1a1,
    d1a2,
    d1b1,
    d1b2,
    table,
    chosen,
    d2_t,
    bd,
    yv,
    rs_send,
    rs_recv,
    dyall,
    ar_part,
    ar_in,
    ar_mid,
    glt,
    lowt,
    lmat,
    term,
    g2_t,
    pieces,
    sums,
    g1_t,
    tu,
    su,
    ug_t,
    gu,
    guv,
    giv,
    valv,
):
    i = lax.axis_index("dp")
    z = lax.axis_index("tensor")
    c = lax.rem(i, NC)
    y = lax.rem(lax.div(i, NC), NY)
    x = lax.div(i, NC * NY)
    sems = Sems(sem_ref)

    def dev(xx=x, yy=y, cc=c, zz=z):
        return ((xx * NY + yy) * NC + cc, zz)

    def turn(v, d, n):
        return lax.rem(v + d, n)

    def remote(src, dst, device):
        copy = pltpu.make_async_remote_copy(
            src_ref=src,
            dst_ref=dst,
            send_sem=sems.take(),
            recv_sem=sems.take(),
            device_id=device,
            device_id_type=MESH,
        )
        copy.start()
        return copy

    def local(src, dst):
        copy = pltpu.make_async_copy(src, dst, sems.take())
        copy.start()
        return copy

    def wait(copies):
        for copy in copies:
            copy.wait()

    def step(axis, src, dst):
        own, size = {"x": (x, NX), "y": (y, NY), "c": (c, NC)}[axis]
        key = {"x": "xx", "y": "yy", "c": "cc"}[axis]
        copies = []
        for d in (2, 1, 3) if size == 4 else (1,):
            to = turn(own, d, size)
            copies.append(remote(src(to), dst(own), dev(**{key: to})))
        copies.append(local(src(own), dst(own)))
        return copies

    class Exchange:
        def __init__(self, slots, mid, out):
            self.slots, self.mid, self.out = slots, mid, out

            self.halves = [[], []]

        def first(self, *halves):
            s, m = self.slots, self.mid
            for h in halves or (0, 1):
                if h == 0:
                    self.halves[0] = step("x", lambda t: s.at[t, :, :, 0], lambda o: m.at[0, o])
                else:
                    self.halves[1] = step("y", lambda t: s.at[:, t, :, 1], lambda o: m.at[1, :, o])

        def second(self):
            m, (one, two) = self.mid, self.halves
            wait(one)
            one = step("y", lambda t: m.at[0, :, t], lambda o: m.at[2, :, o])
            wait(two)
            self.halves = one, step("x", lambda t: m.at[1, t], lambda o: m.at[3, o])

        def third(self):
            m, out, (one, two) = self.mid, self.out, self.halves
            wait(one)
            one = step("c", lambda t: m.at[2, :, :, t], lambda o: out.at[:, :, o, 0])
            wait(two)
            two = step("c", lambda t: m.at[3, :, :, t], lambda o: out.at[:, :, o, 1])
            self.copies = one + two

        def finish(self):
            wait(self.copies)

    def lanes(k, width):
        return pl.ds(pl.multiple_of(k * width, width), width)

    class Down:
        def first(self):
            self.one = step(
                "x",
                lambda t: d_hbm.at[pl.ds(0, 8), :, :, :, lanes(t, 256)],
                lambda o: d1a1.at[o],
            )
            self.two = step("y", lambda t: d_hbm.at[pl.ds(8, 8), t], lambda o: d1b1.at[o])

        def second(self):
            wait(self.two)
            self.two = step(
                "x", lambda t: d1b1.at[:, :, :, :, lanes(t, 256)], lambda o: d1b2.at[o]
            )
            wait(self.one)
            self.one = step("y", lambda t: d1a1.at[:, :, t], lambda o: d1a2.at[:, o])

        def third(self):
            wait(self.two)
            self.two = step("c", lambda t: d1b2.at[:, :, :, t], lambda o: table.at[o, 1])
            wait(self.one)
            self.one = step("c", lambda t: d1a2.at[:, :, :, t], lambda o: table.at[o, 0])

        def finish(self):
            wait(self.one + self.two)

    class Gather:
        def slot(self, k):
            return dyall.at[lax.div(k, 2), :, lanes(lax.rem(k, 2), BLOCK)]

        def start(self, s):
            self.copies = []
            for d, last in ((1, 4), (NZ - 1, 3)):
                if s < last:
                    k = turn(z, (NZ - d) * s, NZ)
                    src = dyv if s == 0 else self.slot(k)
                    self.copies.append(remote(src, self.slot(k), dev(zz=turn(z, d, NZ))))
            if s == 0:
                self.own = local(dyv, self.slot(z))

        def finish(self, s):
            wait(self.copies)
            if s == 0:
                self.own.wait()

    class Scatter:
        def start(self, s):
            if s:
                wait(self.copies)
            self.copies = []
            for way, (d, last) in enumerate(((1, 4), (NZ - 1, 3))):
                if s < last:
                    own = yv[turn(z, d * (last - s), NZ)]
                    if s:
                        own = own + rs_recv[way, s - 1].astype(f32)
                    rs_send[way, s] = own.astype(bf16)
                    self.copies.append(
                        remote(rs_send.at[way, s], rs_recv.at[way, s], dev(zz=turn(z, d, NZ)))
                    )

        def finish(self):
            wait(self.copies)

    class Reduce:
        def __init__(self, k, out, scale):
            self.k, self.out, self.scale = k, out, scale

        def first(self):
            k = self.k
            self.copies = [
                remote(
                    ar_part.at[k, turn(z, d, NZ)],
                    ar_in.at[k, d - 1],
                    dev(zz=turn(z, d, NZ)),
                )
                for d in range(1, NZ)
            ]

        def second(self):
            k = self.k
            wait(self.copies)
            total = ar_part[k, z]
            for d in range(1, NZ):
                total = total + ar_in[k, d - 1]
            ar_mid[k] = (total * self.scale).astype(bf16)
            self.copies = [
                remote(ar_mid.at[k], self.out.at[z], dev(zz=turn(z, d, NZ))) for d in range(1, NZ)
            ] + [local(ar_mid.at[k], self.out.at[z])]

        def finish(self):
            wait(self.copies)

    barrier = pltpu.get_barrier_semaphore()
    peers = [dev(xx=turn(x, d, NX)) for d in range(1, NX)]
    peers += [dev(yy=turn(y, d, NY)) for d in range(1, NY)]
    peers += [dev(cc=turn(c, 1, NC))]
    peers += [dev(zz=turn(z, d, NZ)) for d in range(1, NZ)]
    for device in peers:
        pl.semaphore_signal(barrier, inc=1, device_id=device, device_id_type=MESH)
    load_dy = local(dy_hbm, dyv)
    load_u = local(u_hbm, uv)
    load_x = local(x_hbm, xv)
    load_w = local(w_hbm, wv)

    lane = lax.broadcasted_iota(i32, (8, 256), 1)
    mine = jnp.zeros((8, 256), i32)
    for b in range(8):
        mine = jnp.where(lane == i * 8 + b, asi[apb[b]], mine)
    spot[0] = mine
    pl.semaphore_wait(barrier, len(peers))

    down = Down()
    gather = Gather()
    scatter = Scatter()

    axes = (("xx", x, NX), ("yy", y, NY), ("cc", c, NC))
    for k, (key, own, size) in enumerate(axes):
        copies = [
            remote(spot.at[k], spot_in.at[3 * k + d - 1], dev(**{key: turn(own, d, size)}))
            for d in range(1, size)
        ]
        if k == 0:
            down.first()
            load_dy.wait()
            gather.start(0)
        wait(copies)
        total = spot[k]
        for d in range(1, size):
            total = total + spot_in[3 * k + d - 1]
        if k < 2:
            spot[k + 1] = total
        else:
            spot_all[...] = total
    local(spot_all, spot_s).wait()

    load_u.wait()

    def reply(k, _):
        found = jnp.int32(0)
        for b in range(8):
            s = spot_s[0, k * 8 + b]
            hit = lax.shift_right_logical(s, 4) == i
            found = jnp.where(hit, lax.bitwise_and(s, 15) + 1, found)
        lu_s[k] = found - 1
        chunk = uv[jnp.maximum(found - 1, 0)]
        ru[lax.div(k, 8), lax.rem(lax.div(k, 2), 4), lax.rem(k, 2)] = chunk
        return 0

    lax.fori_loop(0, DP, reply, 0)
    up = Exchange(ru, u_t, fu)
    up.first()
    down.second()
    gather.finish(0)
    gather.start(1)

    load_x.wait()
    load_w.wait()

    def base(n, _):
        part = nn(xv[...], wv[:, lanes(n, 256)])
        yv[2 * n] = part[:, :BLOCK]
        yv[2 * n + 1] = part[:, BLOCK:]
        return 0

    lax.fori_loop(0, 4, base, 0)
    up.second()
    gather.finish(1)
    gather.start(2)
    up.third()
    up.finish()

    for b in range(8):
        k = lax.shift_right_logical(spot_s[0, i * 8 + b], 4)
        chunk = fu[
            lax.shift_right_logical(k, 3),
            lax.bitwise_and(lax.shift_right_logical(k, 1), 3),
            lax.bitwise_and(k, 1),
        ]
        ub[b] = chunk.reshape(64, BLOCK)
    for b in range(8):
        ar_part[0, b] = nt(ub[b], dyv[b * BLOCK : (b + 1) * BLOCK])
    grad_low = Reduce(0, glt, adapter_scale)
    grad_low.first()
    down.third()
    grad_low.second()
    down.finish()

    fetch = Exchange(chosen, d2_t, bd)
    for h in range(2):

        def choose(k, _):
            for b in range(4):
                s = spot_s[0, k * 8 + h * 4 + b]
                piece = table[
                    lax.bitwise_and(lax.shift_right_logical(s, 4), 1),
                    lax.bitwise_and(lax.shift_right_logical(s, 3), 1),
                    lax.shift_right_logical(s, 7),
                    lax.bitwise_and(lax.shift_right_logical(s, 5), 3),
                    lax.bitwise_and(s, 7),
                ]
                chosen[lax.div(k, 8), lax.rem(lax.div(k, 2), 4), lax.rem(k, 2), h, b] = piece
            return 0

        lax.fori_loop(0, DP, choose, 0)
        fetch.first(h)

    grad_low.finish()
    row = lax.broadcasted_iota(i32, (512, 64), 0)
    col = lax.broadcasted_iota(i32, (512, 64), 1)
    for b in range(8):
        spread = (row == col * 8 + b).astype(f32).astype(bf16)
        lmat[:, b * BLOCK : (b + 1) * BLOCK] = nn(spread, glt[b]).astype(bf16)

    def terms(n, _):
        part = nn(lmat[...], xv[:, lanes(n, 256)])
        term[:, :, :, :, :, lanes(n, 256)] = part.reshape(4, 4, 2, 2, 8, 256).astype(bf16)
        return 0

    lax.fori_loop(0, 4, terms, 0)
    give = Exchange(term, g2_t, pieces)
    give.first()
    gather.finish(2)
    gather.start(3)
    fetch.second()
    pick = (lax.broadcasted_iota(i32, (512, 256), 0) == spot_all[0:1, :]).astype(f32).astype(bf16)
    give.second()
    fetch.third()
    gather.finish(3)
    scatter.start(0)
    fetch.finish()

    for b in range(8):
        part = jnp.zeros((64, BLOCK), f32)
        for q in range(4):
            mat = bd[q, :, :, b // 4, b % 4].reshape(64, 256)
            part = part + nt(mat, xv[b * BLOCK : (b + 1) * BLOCK, q * 256 : (q + 1) * 256])
        ar_part[1, b] = part
    low = Reduce(1, lowt, 1.0)
    low.first()
    give.third()
    give.finish()

    keep = Exchange(sums, g1_t, gd_out)
    for h in range(2):

        def add(n, _):
            mat = pieces[:, :, :, h, :, lanes(n, 256)].reshape(256, 256)
            part = nn(pick, mat).astype(bf16)
            sums[:, :, :, h, :, lanes(n, 256)] = part.reshape(4, 4, 2, 16, 256)
            return 0

        lax.fori_loop(0, 4, add, 0)
        keep.first(h)

    low.second()
    scatter.start(1)
    low.finish()
    for b in range(8):
        tu[b] = nn(lowt[b], dyv[b * BLOCK : (b + 1) * BLOCK]).astype(bf16).reshape(2, 32, BLOCK)

    def send_up(k, _):
        found = jnp.int32(0)
        for b in range(8):
            hit = lax.shift_right_logical(spot_s[0, i * 8 + b], 4) == k
            found = jnp.where(hit, b + 1, found)
        chunk = tu[jnp.maximum(found - 1, 0)].astype(f32)
        chunk = jnp.where(found > 0, chunk, 0.0)
        su[lax.div(k, 8), lax.rem(lax.div(k, 2), 4), lax.rem(k, 2)] = chunk.astype(bf16)
        return 0

    lax.fori_loop(0, DP, send_up, 0)
    give_up = Exchange(su, ug_t, gu)
    give_up.first()
    def backward(n, _):
        part = jnp.zeros((1024, 256), f32)
        for k in range(4):
            part = part + nt(dyall[k], wv[lanes(n, 256), k * 256 : (k + 1) * 256])
        for b in range(8):
            rows = slice(b * BLOCK, (b + 1) * BLOCK)
            mat = bd[n, :, :, b // 4, b % 4].reshape(64, 256)
            giv[rows, lanes(n, 256)] = (part[rows] + tn(glt[b], mat)).astype(bf16)
        return 0

    lax.fori_loop(0, 4, backward, 0)
    store_gi = local(giv, gi_out)
    scatter.start(2)
    give_up.second()
    keep.second()

    give_up.third()
    scatter.start(3)
    give_up.finish()

    def add_up(k, _):
        total = jnp.zeros((2, 32, BLOCK), f32)
        for j in range(DP):
            share = jnp.where(lu_s[j] == k, 1.0, 0.0).astype(f32)
            total = total + gu[j // 8, (j // 2) % 4, j % 2].astype(f32) * share
        guv[k] = total.astype(bf16)
        return 0

    lax.fori_loop(0, 16, add_up, 0)
    store_gu = local(guv, gu_out)
    scatter.finish()
    for b in range(8):
        rows = slice(b * BLOCK, (b + 1) * BLOCK)
        frozen = yv[z, rows] + rs_recv[0, 3, rows].astype(f32) + rs_recv[1, 2, rows].astype(f32)
        valv[rows] = (frozen + adapter_scale * tn(lowt[b], ub[b])).astype(bf16)
    store_values = local(valv, values_out)
    keep.third()
    keep.finish()
    wait([store_gi, store_gu, store_values])
    assert sems.used <= sem_ref.shape[0], sems.used


def on_device(inputs, frozen, down, up, apb, asi, dy):
    any_ = pl.BlockSpec(memory_space=pl.ANY)
    smem = pl.BlockSpec(memory_space=pltpu.SMEM)

    def v(*shape, dtype=bf16):
        return pltpu.VMEM(shape, dtype)

    values, grad_inputs, gd, gu = pl.pallas_call(
        kernel,
        out_shape=(
            jax.ShapeDtypeStruct((1024, 128), bf16),
            jax.ShapeDtypeStruct((1024, 1024), bf16),
            jax.ShapeDtypeStruct((4, 4, 2, 2, 16, 1024), bf16),
            jax.ShapeDtypeStruct((16, 2, 32, 128), bf16),
        ),
        in_specs=[smem, smem, any_, any_, any_, any_, any_],
        out_specs=(any_,) * 4,
        scratch_shapes=[
            pltpu.SemaphoreType.DMA((340,)),
            v(1024, 1024),
            v(1024, 1024),
            v(16, 2, 32, 128),
            v(1024, 128),
            v(3, 8, 256, dtype=i32),
            v(7, 8, 256, dtype=i32),
            v(8, 256, dtype=i32),
            pltpu.SMEM((8, 256), i32),
            pltpu.SMEM((32,), i32),
            v(4, 4, 2, 2, 32, 128),
            v(4, 4, 4, 2, 32, 128),
            v(4, 4, 2, 2, 32, 128),
            v(8, 64, 128),
            v(4, 8, 4, 2, 8, 256),
            v(4, 4, 8, 2, 8, 256),
            v(4, 8, 2, 8, 1024),
            v(4, 4, 8, 2, 8, 256),
            v(2, 2, 4, 4, 8, 8, 256),
            v(4, 4, 2, 2, 4, 8, 256),
            v(4, 4, 4, 2, 4, 8, 256),
            v(4, 4, 2, 2, 4, 8, 256),
            v(8, 1024, 128, dtype=f32),
            v(2, 4, 1024, 128),
            v(2, 4, 1024, 128),
            v(4, 1024, 256),
            v(2, 8, 64, 128, dtype=f32),
            v(2, 7, 64, 128, dtype=f32),
            v(2, 64, 128),
            v(8, 64, 128),
            v(8, 64, 128),
            v(512, 1024),
            v(4, 4, 2, 2, 8, 1024),
            v(4, 4, 4, 2, 8, 1024),
            v(4, 4, 2, 2, 8, 1024),
            v(4, 4, 2, 2, 16, 1024),
            v(4, 4, 4, 2, 16, 1024),
            v(8, 2, 32, 128),
            v(4, 4, 2, 2, 32, 128),
            v(4, 4, 4, 2, 32, 128),
            v(4, 4, 2, 2, 32, 128),
            v(16, 2, 32, 128),
            v(1024, 1024),
            v(1024, 128),
        ],
        compiler_params=pltpu.CompilerParams(
            collective_id=0, has_side_effects=True, vmem_limit_bytes=60 * 2**20
        ),
    )(
        apb,
        asi,
        inputs,
        frozen,
        down.swapaxes(1, 2).reshape(16, 4, 2, 8, 1024),
        up.reshape(16, 2, 32, 128),
        dy,
    )
    grad_down = gd.reshape(64, 16, 1024).transpose(1, 2, 0)
    return values, grad_inputs, grad_down, gu.reshape(16, 64, 128)


def solution(mesh):
    return jax.shard_map(
        on_device,
        mesh=mesh,
        in_specs=(
            P("dp", "tensor"),
            P("tensor", None),
            P("dp", "tensor", None),
            P("dp", None, "tensor"),
            P("dp"),
            P(),
            P("dp", "tensor"),
        ),
        out_specs=(
            P("dp", "tensor"),
            P("dp", "tensor"),
            P("dp", "tensor", None),
            P("dp", None, "tensor"),
        ),
        check_vma=False,
    )
```
